32 devices in a mesh: grp: 2 (over x), kv: 16 (over z, y, core).
Axes of the slice: x: 2, y: 2, z: 4, core: 2. Of those that a mesh axis runs over, the one named last changes fastest.
Arguments:
- queries: bfloat16 [32, 8192], P(('grp', 'kv')), parts along dimension 0, may hold values from -40 to 40
- stored_keys: bfloat16 [65536, 1024], P(('grp', 'kv')), parts along dimension 0, may hold values from -4.5 to 4.5
- stored_values: bfloat16 [65536, 1024], P(('grp', 'kv')), parts along dimension 0, may hold values from -6 to 6
- kv_counts: int32 [32], P(('grp', 'kv')), parts along dimension 0, may hold values from 1 to 2048, 20480 in all
Outputs:
- attended: bfloat16 [32, 8192], P(('grp', 'kv')), parts along dimension 0
The draws below stay inside these ranges and needn't reach their ends.
There are 2 independent parts, one for each index of `grp`. The reference program is written for one: setup_inputs(seed, part) draws one part's arguments, and reference() takes and returns one part's arrays. A program takes and returns all parts, laid end to end along the dimension named above; each array names one. Nothing has to cross between parts.
Inputs may be any that keep to these rules, and one draw needn't show every extreme that they name: `kv_counts`: every shard has a live slot; the fullest shard has all 2048 slots live; the counts sum to 16 * 2048 * 5 // 8.
All inputs are finite; a program needn't handle non-finite values.
Results may differ from the reference program's by a relative error of at most 0.0085.
Values may be sent and summed in bfloat16 or wider, within the bound.
A program may use at most 64 MiB of HBM per device.

```python
import math
import jax
import jax.numpy as jnp
import numpy as np
from jax import lax

QUERY_HEADS = 64
KEY_VALUE_HEADS = 8
HEAD_DIM = 128
SHARD_CAPACITY = 2048
FRESH_TOKENS = 16
CONTEXT_SLOTS = 32768
N_KV = 16


def key_matrix(key):
    token_rows = N_KV * SHARD_CAPACITY
    seed_key = jax.random.fold_in(key, 11)
    value_matrix = jnp.clip(jax.random.normal(seed_key, (token_rows, KEY_VALUE_HEADS * HEAD_DIM), jnp.float32), -4.5, 4.5)
    return value_matrix


def draw_stored_keys(key, part):
    return key_matrix(key).astype(jnp.bfloat16)


def draw_queries(key, part):
    query_key = jax.random.fold_in(key, 21)
    base = jnp.clip(4.0 * jax.random.normal(query_key, (FRESH_TOKENS, QUERY_HEADS * HEAD_DIM), jnp.float32), -24.0, 24.0)
    return base.astype(jnp.bfloat16)


def block_scale(own_key, shape, shards, low, top_value):
    def one(dim, shards_of):
        heights = jax.random.uniform(jax.random.fold_in(jax.random.fold_in(own_key, 6), dim), (shards_of,), jnp.float32, low / len(shards), top_value / len(shards))
        return jnp.repeat(jnp.exp(heights), shape[dim] // shards_of).reshape((-1,) + (1,) * (len(shape) - dim - 1))

    level = one(*shards[0])
    for cut in shards[1:]:
        level = level * one(*cut)
    return level


def profile(number_of, total, reach, skew):
    weights = [(1 << 20) // math.isqrt(standing ** skew) + 1 for standing in range(2, number_of + 1)]
    spare, counts = total - reach - (number_of - 1), [1] * (number_of - 1)
    while spare > 0:
        candidates = [i for i in range(number_of - 1) if counts[i] < reach]
        whole, left = sum([weights[i] for i in candidates]), spare
        for i in candidates:
            more = min(reach - counts[i], max(1, left * weights[i] // whole), spare)
            counts[i] = counts[i] + more
            spare = spare - more
    return np.array([reach] + counts)


def uneven(stream_key, count, total, bound, skew):
    if count == 2:
        one = jax.random.randint(stream_key, (), max(1, total - bound), min(bound, total - 1) + 1)
        return jnp.stack([one, total - one])
    sizes = jnp.asarray(profile(count, total, bound, skew), jnp.int32)
    pairs = (count - 1) // 2
    source_of, sink = sizes[1:1 + 2 * pairs:2], sizes[2:2 + 2 * pairs:2]
    slack = jnp.minimum(source_of - 1, bound - sink)
    shifted = jax.random.randint(jax.random.fold_in(stream_key, 1), (pairs,), 0, 1 << 20) % (slack + 1)
    sizes = sizes.at[1:1 + 2 * pairs:2].set(source_of - shifted).at[2:2 + 2 * pairs:2].set(sink + shifted)
    return sizes[jax.random.permutation(jax.random.fold_in(stream_key, 2), count)]


def normal_values(rng, shape, spread, bound, split=(), held_as=jnp.bfloat16):
    drawn = jax.random.normal(rng, shape, jnp.float32) * spread
    if len(split) > 0:
        drawn = block_scale(rng, shape, split, -0.22, 0.18) * drawn
    return jnp.clip(drawn, min=-bound, max=bound).astype(held_as)


def setup_inputs(seed: int = 0, part: int = 0) -> dict:
    arg_keys = jax.random.split(jax.random.key(seed), 5)
    part_splits = jax.random.split(jax.random.fold_in(arg_keys[4], part), 5)
    queries = draw_queries(jax.random.fold_in(jax.random.fold_in(arg_keys[4], part), 71), part)
    stored_keys = draw_stored_keys(jax.random.fold_in(jax.random.fold_in(arg_keys[4], part), 71), part)
    stored_values = normal_values(part_splits[2], (CONTEXT_SLOTS, KEY_VALUE_HEADS * HEAD_DIM), 1.0, 6.0, ((0, 16),))
    kv_counts = uneven(part_splits[3], N_KV, N_KV * SHARD_CAPACITY * 5 // 8, SHARD_CAPACITY, 2).astype(jnp.int32)
    return {"queries": queries, "stored_keys": stored_keys, "stored_values": stored_values, "kv_counts": kv_counts}


def shard_terms(grouped_query, keys, values, live_count):
    inv_root = HEAD_DIM ** -0.5
    scores = jnp.einsum('gnd,sgd->gns', grouped_query, keys.astype(jnp.float32)) * inv_root
    live_mask = jnp.arange(SHARD_CAPACITY) < live_count
    scores = jnp.where(live_mask, scores, -1e30)
    partial_maxima = jnp.max(scores, axis=2)
    probas = jnp.where(live_mask, jnp.exp(scores - partial_maxima[..., None]), 0.0).astype(jnp.bfloat16)
    partial_denominator = jnp.sum(probas.astype(jnp.float32), axis=2)
    partial_output = jnp.einsum('gns,sgd->gnd', probas.astype(jnp.float32), values.astype(jnp.float32))
    shard_part = (partial_output / partial_denominator[..., None]).astype(jnp.bfloat16)
    shard_part = lax.optimization_barrier(shard_part).astype(jnp.float32)
    return partial_maxima, partial_denominator, shard_part


def reference(queries, stored_keys, stored_values, kv_counts):
    group_ratio = QUERY_HEADS // KEY_VALUE_HEADS
    grouped_query = queries.astype(jnp.float32).reshape(FRESH_TOKENS, KEY_VALUE_HEADS, group_ratio, HEAD_DIM)
    grouped_query = grouped_query.transpose(1, 0, 2, 3).reshape(KEY_VALUE_HEADS, FRESH_TOKENS * group_ratio, HEAD_DIM)
    full_keys = stored_keys.reshape(N_KV, SHARD_CAPACITY, KEY_VALUE_HEADS, HEAD_DIM)
    full_values = stored_values.reshape(N_KV, SHARD_CAPACITY, KEY_VALUE_HEADS, HEAD_DIM)

    def advance(state_now, inputs):
        row_top, denom_sum, combined = state_now
        keys, values, live_count = inputs
        partial_maxima, partial_denominator, shard_part = shard_terms(grouped_query, keys, values, live_count)
        new_top = jnp.maximum(row_top, partial_maxima)
        old_weight = jnp.exp(row_top - new_top)
        new_weight = jnp.exp(partial_maxima - new_top) * partial_denominator
        denom_sum = denom_sum * old_weight + new_weight
        combined = combined * old_weight[..., None] + shard_part * new_weight[..., None]
        return (new_top, denom_sum, combined), None

    offset_position = (jnp.full((KEY_VALUE_HEADS, FRESH_TOKENS * group_ratio), -1e30, jnp.float32),
             jnp.zeros((KEY_VALUE_HEADS, FRESH_TOKENS * group_ratio), jnp.float32),
             jnp.zeros((KEY_VALUE_HEADS, FRESH_TOKENS * group_ratio, HEAD_DIM), jnp.float32))
    final, unused = lax.scan(advance, offset_position, (full_keys, full_values, kv_counts.astype(jnp.int32)))
    row_top, denom_sum, combined = final
    attention_output = combined / denom_sum[..., None]
    attention_output = attention_output.reshape(KEY_VALUE_HEADS, FRESH_TOKENS, group_ratio, HEAD_DIM).transpose(1, 0, 2, 3).reshape(FRESH_TOKENS, QUERY_HEADS * HEAD_DIM)
    return attention_output.astype(jnp.bfloat16)
```

```python
import functools
import math

import jax
import jax.numpy as jnp
from jax import lax
from jax.experimental import pallas as pl
from jax.experimental.pallas import tpu as pltpu
from jax.sharding import PartitionSpec as P

QUERY_HEADS = 64
KEY_VALUE_HEADS = 8
HEAD_DIM = 128
RATIO = QUERY_HEADS // KEY_VALUE_HEADS
FIRST = (0, 2, 6)
SIZE = (2, 4, 2)
PAIRS = len(SIZE)
TILE = 512
SCALE2 = HEAD_DIM ** (-0.5) * math.log2(math.e)
MESH = pl.DeviceIdType.MESH


def kernel(n, count_ref, q_hbm, k_hbm, v_hbm, out_ref,
           q_flat, q_rows, q_own, out_rows, k_buf, v_buf, q_buf,
           send_part, send_stat, pair_part, pair_stat,
           out_part, out_stat, out_row, recv_part, recv_row, s_buf,
           in_sem, k_sem, v_sem, q_send, q_recv, f_send, f_recv,
           x_send, x_recv, y_send, y_recv, p_send, p_recv, s_send, s_recv):
    me = lax.axis_index("kv")
    core = lax.rem(me, 2)
    chip = lax.div(me, 2)
    chips = n // 2
    sibling = me + 1 - 2 * core
    slots = k_buf.shape[1]
    block = min(chips, 8)

    def fetch(k):
        copies = []
        for g in range(FIRST[k], FIRST[k] + SIZE[k]):
            columns = pl.ds(g * HEAD_DIM, HEAD_DIM)
            copies.append(pltpu.make_async_copy(k_hbm.at[:, columns], k_buf.at[g], k_sem.at[g]))
            copies.append(pltpu.make_async_copy(v_hbm.at[:, columns], v_buf.at[g], v_sem.at[g]))
        return copies

    def rows(k):
        return pl.ds(FIRST[k] * RATIO, SIZE[k] * RATIO)

    def to(device, src, dst, send, recv):
        return pltpu.make_async_remote_copy(
            src_ref=src, dst_ref=dst, send_sem=send, recv_sem=recv,
            device_id={"kv": device}, device_id_type=MESH)

    def each_chip(body):
        def step(d, carry):
            other = lax.rem(chip + d, chips)
            body(other, 2 * other + core)
            return carry
        lax.fori_loop(1, chips, step, 0)

    def blocks(body):
        if chips == block:
            body(0)
        else:
            def step(b, carry):
                body(b)
                return carry
            lax.fori_loop(0, chips // block, step, 0)

    q_in = pltpu.make_async_copy(q_hbm, q_flat, in_sem.at[0])
    q_in.start()
    barrier = pltpu.get_barrier_semaphore()

    def signal(device):
        pl.semaphore_signal(barrier, inc=1, device_id={"kv": device}, device_id_type=MESH)

    each_chip(lambda other, device: signal(device))
    signal(sibling)
    for k in range(PAIRS):
        for copy in fetch(k):
            copy.start()

    q_in.wait()
    for h in range(QUERY_HEADS):
        q_rows[h:h + 1, :] = q_flat[:, h * HEAD_DIM:(h + 1) * HEAD_DIM].astype(jnp.float32)
    own = q_rows[...].astype(jnp.bfloat16)
    q_own[...] = own
    q_buf[core, chip] = own
    live = lax.broadcasted_iota(jnp.int32, (1, slots), 1) < count_ref[0]
    out_stat[...] = jnp.zeros_like(out_stat)
    pl.semaphore_wait(barrier, chips)

    for k in range(PAIRS):
        each_chip(lambda other, device: to(
            device, q_own.at[rows(k)], q_buf.at[core, chip, rows(k)],
            q_send.at[k], q_recv.at[k]).start())

    def whole(buf, k, sem):
        part = buf.at[pl.ds(0, chips - 1), rows(k)]
        return pltpu.make_async_copy(part, part, sem.at[k])

    def forward(k):
        part = q_buf.at[core, :, rows(k)]
        return to(sibling, part, part, f_send.at[k], f_recv.at[k])

    def swap_part(k):
        return to(sibling, send_part.at[1 - core, :, rows(k)], pair_part.at[:, rows(k)],
                  x_send.at[k], x_recv.at[k])

    def swap_stat(k):
        return to(sibling, send_stat.at[1 - core, :, rows(k)], pair_stat.at[:, rows(k)],
                  y_send.at[k], y_recv.at[k])

    def take(k):
        whole(q_buf.at[core], k, q_recv).wait()
        forward(k).start()

    count = 2 * block * RATIO

    def compute(k):
        def one(b):
            group = pl.ds(b * block, block)
            parts = []
            stats = []
            peaks = []
            for half in range(SIZE[k]):
                g = FIRST[k] + half
                q = q_buf[:, group, g * RATIO:(g + 1) * RATIO, :].astype(jnp.float32)
                q = q.reshape(count, HEAD_DIM).astype(jnp.bfloat16)
                peak = jnp.full((count, HEAD_DIM), -1e30, jnp.float32)
                for c in range(0, slots, TILE):
                    s = lax.dot_general(q, k_buf[g, c:c + TILE], (((1,), (1,)), ((), ())),
                                        preferred_element_type=jnp.float32)
                    s = jnp.where(live[:, c:c + TILE], s, -1e30)
                    s_buf[half, :, c:c + TILE] = s
                    for d in range(0, TILE, HEAD_DIM):
                        peak = jnp.maximum(peak, s[:, d:d + HEAD_DIM])
                peaks.append(jnp.max(peak, axis=1, keepdims=True) * SCALE2)
            for half in range(SIZE[k]):
                g = FIRST[k] + half
                top = peaks[half]
                total = jnp.zeros((count, HEAD_DIM), jnp.float32)
                o = jnp.zeros((count, HEAD_DIM), jnp.float32)
                for c in range(0, slots, TILE):
                    p = jnp.exp2(s_buf[half, :, c:c + TILE] * SCALE2 - top)
                    for d in range(0, TILE, HEAD_DIM):
                        total = total + p[:, d:d + HEAD_DIM]
                    o = o + jnp.dot(p.astype(jnp.bfloat16), v_buf[g, c:c + TILE],
                                    preferred_element_type=jnp.float32)
                total = jnp.broadcast_to(jnp.sum(total, axis=1, keepdims=True), o.shape)
                parts.append((o / total).reshape(2, block, RATIO, HEAD_DIM))
                stats.append((top + jnp.log2(total)).reshape(2, block, RATIO, HEAD_DIM))
            send_part[:, group, rows(k), :] = jnp.concatenate(parts, axis=2).astype(jnp.bfloat16)
            send_stat[:, group, rows(k), :] = jnp.concatenate(stats, axis=2)

        blocks(one)
        swap_part(k).start()
        swap_stat(k).start()

    shape = (block, RATIO, HEAD_DIM)
    lane = lax.broadcasted_iota(jnp.int32, shape, 2)
    row = lax.broadcasted_iota(jnp.int32, shape, 1)

    def merge(k):
        swap_part(k).wait_recv()
        swap_stat(k).wait_recv()

        def one(b):
            group = pl.ds(b * block, block)
            a = send_part[core, group, rows(k), :].astype(jnp.float32)
            c = pair_part[group, rows(k), :].astype(jnp.float32)
            la = send_stat[core, group, rows(k), :]
            lc = pair_stat[group, rows(k), :]
            top = jnp.maximum(la, lc)
            wa = jnp.exp2(la - top)
            wc = jnp.exp2(lc - top)
            total = wa + wc
            out_part[group, rows(k), :] = ((wa * a + wc * c) / total).astype(jnp.bfloat16)
            lse = top + jnp.log2(total)
            stat = out_stat[group]
            for half in range(SIZE[k]):
                g = FIRST[k] + half
                stat = jnp.where(lane == g * RATIO + row, lse[:, half * RATIO:(half + 1) * RATIO, :], stat)
            if k < PAIRS - 1:
                out_stat[group] = stat
            else:
                out_row[group] = jnp.sum(stat, axis=1, keepdims=True)

        blocks(one)
        each_chip(lambda other, device: to(
            device, out_part.at[other, rows(k)], recv_part.at[chip, rows(k)],
            p_send.at[k], p_recv.at[k]).start())
        if k == PAIRS - 1:
            each_chip(lambda other, device: to(
                device, out_row.at[other], recv_row.at[chip],
                s_send.at[0], s_recv.at[0]).start())

    take(0)
    take(1)
    for k in range(PAIRS):
        forward(k).wait_recv()
        for copy in fetch(k):
            copy.wait()
        compute(k)
        if k + 2 < PAIRS:
            take(k + 2)
        if k > 0:
            merge(k - 1)
    merge(PAIRS - 1)
    recv_part[chip] = out_part[chip]
    recv_row[chip] = out_row[chip]

    def row_bytes(sem):
        part = recv_row.at[pl.ds(0, chips - 1)]
        return pltpu.make_async_copy(part, part, sem.at[0])

    for k in range(PAIRS):
        whole(recv_part, k, p_recv).wait()
    row_bytes(s_recv).wait()

    lse = recv_row[...]
    weight = jnp.exp2(lse - jnp.max(lse, axis=0, keepdims=True))
    recv_row[...] = weight / jnp.sum(weight, axis=0, keepdims=True)
    lane2 = lax.broadcasted_iota(jnp.int32, (RATIO, HEAD_DIM), 1)
    row2 = lax.broadcasted_iota(jnp.int32, (RATIO, HEAD_DIM), 0)

    def add(j, acc):
        w = jnp.broadcast_to(recv_row[j], (RATIO, HEAD_DIM))
        x = recv_part[j].astype(jnp.float32)
        new = []
        for g in range(KEY_VALUE_HEADS):
            col = jnp.sum(jnp.where(lane2 == g * RATIO + row2, w, 0.0), axis=1, keepdims=True)
            new.append(acc[g] + col * x[g * RATIO:(g + 1) * RATIO, :])
        return tuple(new)

    zero = jnp.zeros((RATIO, HEAD_DIM), jnp.float32)
    acc = lax.fori_loop(0, chips, add, (zero,) * KEY_VALUE_HEADS, unroll=block)
    out_rows[...] = jnp.concatenate(acc, axis=0)
    for h in range(QUERY_HEADS):
        out_ref[:, h * HEAD_DIM:(h + 1) * HEAD_DIM] = out_rows[h:h + 1, :].astype(out_ref.dtype)

    for k in range(PAIRS):
        whole(q_buf.at[core], k, q_send).wait()
        whole(recv_part, k, p_send).wait()
        forward(k).wait_send()
        swap_part(k).wait_send()
        swap_stat(k).wait_send()
    row_bytes(s_send).wait()


def solution(mesh):
    n = mesh.shape["kv"]

    def body(queries, stored_keys, stored_values, kv_counts):
        slots = stored_keys.shape[0]
        chips = n // 2
        hbm = pl.BlockSpec(memory_space=pltpu.HBM)
        part = (chips, QUERY_HEADS, HEAD_DIM)
        both = (2,) + part
        dma = pltpu.SemaphoreType.DMA
        f32, b16 = jnp.float32, jnp.bfloat16
        return pl.pallas_call(
            functools.partial(kernel, n),
            out_shape=jax.ShapeDtypeStruct(queries.shape, b16),
            in_specs=[pl.BlockSpec(memory_space=pltpu.SMEM), hbm, hbm, hbm],
            out_specs=pl.BlockSpec(memory_space=pltpu.VMEM),
            scratch_shapes=[
                pltpu.VMEM(queries.shape, b16),
                pltpu.VMEM((QUERY_HEADS, HEAD_DIM), f32),
                pltpu.VMEM((QUERY_HEADS, HEAD_DIM), b16),
                pltpu.VMEM((QUERY_HEADS, HEAD_DIM), f32),
                pltpu.VMEM((KEY_VALUE_HEADS, slots, HEAD_DIM), b16),
                pltpu.VMEM((KEY_VALUE_HEADS, slots, HEAD_DIM), b16),
                pltpu.VMEM(both, b16),
                pltpu.VMEM(both, b16),
                pltpu.VMEM(both, f32),
                pltpu.VMEM(part, b16),
                pltpu.VMEM(part, f32),
                pltpu.VMEM(part, b16),
                pltpu.VMEM((chips, RATIO, HEAD_DIM), f32),
                pltpu.VMEM((chips, 1, HEAD_DIM), f32),
                pltpu.VMEM(part, b16),
                pltpu.VMEM((chips, 1, HEAD_DIM), f32),
                pltpu.VMEM((4, 2 * min(chips, 8) * RATIO, slots), f32),
                dma((1,)),
            ] + [dma((KEY_VALUE_HEADS,))] * 2 + [dma((PAIRS,))] * 10 + [dma((1,))] * 2,
            compiler_params=pltpu.CompilerParams(
                collective_id=0, has_side_effects=True, vmem_limit_bytes=40 << 20),
        )(kv_counts, *[pltpu.with_memory_space_constraint(x, pltpu.HBM)
                       for x in (queries, stored_keys, stored_values)])

    return jax.shard_map(
        body,
        mesh=mesh,
        in_specs=(
            P(("grp", "kv"), None),
            P(("grp", "kv"), None),
            P(("grp", "kv"), None),
            P(("grp", "kv")),
        ),
        out_specs=P(("grp", "kv"), None),
        check_vma=False,
    )
```

```python
import functools
import math

import jax
import jax.numpy as jnp
from jax import lax
from jax.experimental import pallas as pl
from jax.experimental.pallas import tpu as pltpu
from jax.sharding import PartitionSpec as P

QUERY_HEADS = 64
KEY_VALUE_HEADS = 8
HEAD_DIM = 128
RATIO = QUERY_HEADS // KEY_VALUE_HEADS
FIRST = (0, 2, 6)
SIZE = (2, 4, 2)
PAIRS = len(SIZE)
TILE = 512
FILL = 256
SCALE2 = HEAD_DIM ** (-0.5) * math.log2(math.e)
MESH = pl.DeviceIdType.MESH


def kernel(n, count_ref, q_hbm, k_hbm, v_hbm, out_ref,
           q_flat, q_rows, q_own, out_rows, k_buf, v_buf, q_buf,
           live_buf, send_part, send_stat, pair_part, pair_stat,
           out_part, out_stat, out_row, recv_part, recv_row, s_buf,
           in_sem, k_sem, v_sem, q_send, q_recv, f_send, f_recv,
           x_send, x_recv, y_send, y_recv, p_send, p_recv, s_send, s_recv):
    me = lax.axis_index("kv")
    core = lax.rem(me, 2)
    chip = lax.div(me, 2)
    chips = n // 2
    sibling = me + 1 - 2 * core
    slots = k_buf.shape[1]
    block = min(chips, 8)

    def fetch(k):
        copies = []
        for g in range(FIRST[k], FIRST[k] + SIZE[k]):
            columns = pl.ds(g * HEAD_DIM, HEAD_DIM)
            copies.append(pltpu.make_async_copy(k_hbm.at[:, columns], k_buf.at[g], k_sem.at[g]))
            copies.append(pltpu.make_async_copy(v_hbm.at[:, columns], v_buf.at[g], v_sem.at[g]))
        return copies

    def rows(k):
        return pl.ds(FIRST[k] * RATIO, SIZE[k] * RATIO)

    def to(device, src, dst, send, recv):
        return pltpu.make_async_remote_copy(
            src_ref=src, dst_ref=dst, send_sem=send, recv_sem=recv,
            device_id={"kv": device}, device_id_type=MESH)

    def each_chip(body):
        def step(d, carry):
            other = lax.rem(chip + d, chips)
            body(other, 2 * other + core)
            return carry
        lax.fori_loop(1, chips, step, 0)

    def blocks(body):
        if chips == block:
            body(0)
        else:
            def step(b, carry):
                body(b)
                return carry
            lax.fori_loop(0, chips // block, step, 0)

    q_in = pltpu.make_async_copy(q_hbm, q_flat, in_sem.at[0])
    q_in.start()
    barrier = pltpu.get_barrier_semaphore()

    def signal(device):
        pl.semaphore_signal(barrier, inc=1, device_id={"kv": device}, device_id_type=MESH)

    each_chip(lambda other, device: signal(device))
    signal(sibling)
    for k in range(PAIRS):
        for copy in fetch(k):
            copy.start()

    q_in.wait()
    for h in range(QUERY_HEADS):
        q_rows[h:h + 1, :] = q_flat[:, h * HEAD_DIM:(h + 1) * HEAD_DIM].astype(jnp.float32)
    own = q_rows[...].astype(jnp.bfloat16)
    q_own[...] = own
    q_buf[core, chip] = own
    limit = count_ref[0]
    live = lax.broadcasted_iota(jnp.int32, (slots, HEAD_DIM), 0) < limit
    live_buf[...] = jnp.where(live, 1.0, 0.0).astype(jnp.bfloat16)
    out_stat[...] = jnp.zeros_like(out_stat)
    pl.semaphore_wait(barrier, chips)

    for k in range(PAIRS):
        each_chip(lambda other, device: to(
            device, q_own.at[rows(k)], q_buf.at[core, chip, rows(k)],
            q_send.at[k], q_recv.at[k]).start())

    def whole(buf, k, sem):
        part = buf.at[pl.ds(0, chips - 1), rows(k)]
        return pltpu.make_async_copy(part, part, sem.at[k])

    def forward(k):
        part = q_buf.at[core, :, rows(k)]
        return to(sibling, part, part, f_send.at[k], f_recv.at[k])

    def swap_part(k):
        return to(sibling, send_part.at[1 - core, :, rows(k)], pair_part.at[:, rows(k)],
                  x_send.at[k], x_recv.at[k])

    def swap_stat(k):
        return to(sibling, send_stat.at[1 - core, :, rows(k)], pair_stat.at[:, rows(k)],
                  y_send.at[k], y_recv.at[k])

    def take(k):
        whole(q_buf.at[core], k, q_recv).wait()
        forward(k).start()

    count = 2 * block * RATIO

    def prepare(k):
        for copy in fetch(k):
            copy.wait()
        for g in range(FIRST[k], FIRST[k] + SIZE[k]):
            spare = jnp.broadcast_to(k_buf[g, 0:1].astype(jnp.float32), (FILL, HEAD_DIM)).astype(jnp.bfloat16)

            def step(i, carry):
                part = pl.ds(pl.multiple_of(i * FILL, FILL), FILL)
                keep = live_buf[part]
                k_buf[g, part] = k_buf[g, part] * keep + spare * (1 - keep)
                v_buf[g, part] = v_buf[g, part] * keep
                return carry

            lax.fori_loop(0, slots // FILL, step, 0)

    def compute(k):
        def one(b):
            group = pl.ds(b * block, block)
            parts = []
            stats = []
            peaks = []
            for half in range(SIZE[k]):
                g = FIRST[k] + half
                q = q_buf[:, group, g * RATIO:(g + 1) * RATIO, :].astype(jnp.float32)
                q = q.reshape(count, HEAD_DIM).astype(jnp.bfloat16)
                peak = jnp.full((count, HEAD_DIM), -1e30, jnp.float32)
                for c in range(0, slots, TILE):
                    s = lax.dot_general(q, k_buf[g, c:c + TILE], (((1,), (1,)), ((), ())),
                                        preferred_element_type=jnp.float32)
                    s_buf[half, :, c:c + TILE] = s
                    for d in range(0, TILE, HEAD_DIM):
                        peak = jnp.maximum(peak, s[:, d:d + HEAD_DIM])
                peaks.append(jnp.max(peak, axis=1, keepdims=True) * SCALE2)
            for half in range(SIZE[k]):
                g = FIRST[k] + half
                top = peaks[half]
                o = jnp.zeros((count, 2 * HEAD_DIM), jnp.float32)
                for c in range(0, slots, TILE):
                    p = jnp.exp2(s_buf[half, :, c:c + TILE] * SCALE2 - top)
                    both = jnp.concatenate([v_buf[g, c:c + TILE], live_buf[c:c + TILE]], axis=1)
                    o = o + jnp.dot(p.astype(jnp.bfloat16), both, preferred_element_type=jnp.float32)
                total = o[:, HEAD_DIM:]
                o = o[:, :HEAD_DIM]
                parts.append((o / total).reshape(2, block, RATIO, HEAD_DIM))
                stats.append((top + jnp.log2(total)).reshape(2, block, RATIO, HEAD_DIM))
            send_part[:, group, rows(k), :] = jnp.concatenate(parts, axis=2).astype(jnp.bfloat16)
            send_stat[:, group, rows(k), :] = jnp.concatenate(stats, axis=2)

        blocks(one)
        swap_part(k).start()
        swap_stat(k).start()

    shape = (block, RATIO, HEAD_DIM)
    lane = lax.broadcasted_iota(jnp.int32, shape, 2)
    row = lax.broadcasted_iota(jnp.int32, shape, 1)

    def merge(k):
        swap_part(k).wait_recv()
        swap_stat(k).wait_recv()

        def one(b):
            group = pl.ds(b * block, block)
            a = send_part[core, group, rows(k), :].astype(jnp.float32)
            c = pair_part[group, rows(k), :].astype(jnp.float32)
            la = send_stat[core, group, rows(k), :]
            lc = pair_stat[group, rows(k), :]
            top = jnp.maximum(la, lc)
            wa = jnp.exp2(la - top)
            wc = jnp.exp2(lc - top)
            total = wa + wc
            out_part[group, rows(k), :] = ((wa * a + wc * c) / total).astype(jnp.bfloat16)
            lse = top + jnp.log2(total)
            stat = out_stat[group]
            for half in range(SIZE[k]):
                g = FIRST[k] + half
                stat = jnp.where(lane == g * RATIO + row, lse[:, half * RATIO:(half + 1) * RATIO, :], stat)
            if k < PAIRS - 1:
                out_stat[group] = stat
            else:
                out_row[group] = jnp.sum(stat, axis=1, keepdims=True)

        blocks(one)
        each_chip(lambda other, device: to(
            device, out_part.at[other, rows(k)], recv_part.at[chip, rows(k)],
            p_send.at[k], p_recv.at[k]).start())
        if k == PAIRS - 1:
            each_chip(lambda other, device: to(
                device, out_row.at[other], recv_row.at[chip],
                s_send.at[0], s_recv.at[0]).start())

    for k in range(PAIRS):
        prepare(k)
    take(0)
    take(1)
    for k in range(PAIRS):
        forward(k).wait_recv()
        compute(k)
        if k + 2 < PAIRS:
            take(k + 2)
        if k > 0:
            merge(k - 1)
    merge(PAIRS - 1)
    recv_part[chip] = out_part[chip]
    recv_row[chip] = out_row[chip]

    def row_bytes(sem):
        part = recv_row.at[pl.ds(0, chips - 1)]
        return pltpu.make_async_copy(part, part, sem.at[0])

    for k in range(PAIRS):
        whole(recv_part, k, p_recv).wait()
    row_bytes(s_recv).wait()

    lse = recv_row[...]
    weight = jnp.exp2(lse - jnp.max(lse, axis=0, keepdims=True))
    recv_row[...] = weight / jnp.sum(weight, axis=0, keepdims=True)
    lane2 = lax.broadcasted_iota(jnp.int32, (RATIO, HEAD_DIM), 1)
    row2 = lax.broadcasted_iota(jnp.int32, (RATIO, HEAD_DIM), 0)

    def add(j, acc):
        w = jnp.broadcast_to(recv_row[j], (RATIO, HEAD_DIM))
        x = recv_part[j].astype(jnp.float32)
        new = []
        for g in range(KEY_VALUE_HEADS):
            col = jnp.sum(jnp.where(lane2 == g * RATIO + row2, w, 0.0), axis=1, keepdims=True)
            new.append(acc[g] + col * x[g * RATIO:(g + 1) * RATIO, :])
        return tuple(new)

    zero = jnp.zeros((RATIO, HEAD_DIM), jnp.float32)
    acc = lax.fori_loop(0, chips, add, (zero,) * KEY_VALUE_HEADS, unroll=block)
    out_rows[...] = jnp.concatenate(acc, axis=0)
    for h in range(QUERY_HEADS):
        out_ref[:, h * HEAD_DIM:(h + 1) * HEAD_DIM] = out_rows[h:h + 1, :].astype(out_ref.dtype)

    for k in range(PAIRS):
        whole(q_buf.at[core], k, q_send).wait()
        whole(recv_part, k, p_send).wait()
        forward(k).wait_send()
        swap_part(k).wait_send()
        swap_stat(k).wait_send()
    row_bytes(s_send).wait()


def solution(mesh):
    n = mesh.shape["kv"]

    def body(queries, stored_keys, stored_values, kv_counts):
        slots = stored_keys.shape[0]
        chips = n // 2
        hbm = pl.BlockSpec(memory_space=pltpu.HBM)
        part = (chips, QUERY_HEADS, HEAD_DIM)
        both = (2,) + part
        dma = pltpu.SemaphoreType.DMA
        f32, b16 = jnp.float32, jnp.bfloat16
        return pl.pallas_call(
            functools.partial(kernel, n),
            out_shape=jax.ShapeDtypeStruct(queries.shape, b16),
            in_specs=[pl.BlockSpec(memory_space=pltpu.SMEM), hbm, hbm, hbm],
            out_specs=pl.BlockSpec(memory_space=pltpu.VMEM),
            scratch_shapes=[
                pltpu.VMEM(queries.shape, b16),
                pltpu.VMEM((QUERY_HEADS, HEAD_DIM), f32),
                pltpu.VMEM((QUERY_HEADS, HEAD_DIM), b16),
                pltpu.VMEM((QUERY_HEADS, HEAD_DIM), f32),
                pltpu.VMEM((KEY_VALUE_HEADS, slots, HEAD_DIM), b16),
                pltpu.VMEM((KEY_VALUE_HEADS, slots, HEAD_DIM), b16),
                pltpu.VMEM(both, b16),
                pltpu.VMEM((slots, HEAD_DIM), b16),
                pltpu.VMEM(both, b16),
                pltpu.VMEM(both, f32),
                pltpu.VMEM(part, b16),
                pltpu.VMEM(part, f32),
                pltpu.VMEM(part, b16),
                pltpu.VMEM((chips, RATIO, HEAD_DIM), f32),
                pltpu.VMEM((chips, 1, HEAD_DIM), f32),
                pltpu.VMEM(part, b16),
                pltpu.VMEM((chips, 1, HEAD_DIM), f32),
                pltpu.VMEM((4, 2 * min(chips, 8) * RATIO, slots), f32),
                dma((1,)),
            ] + [dma((KEY_VALUE_HEADS,))] * 2 + [dma((PAIRS,))] * 10 + [dma((1,))] * 2,
            compiler_params=pltpu.CompilerParams(
                collective_id=0, has_side_effects=True, vmem_limit_bytes=40 << 20),
        )(kv_counts, *[pltpu.with_memory_space_constraint(x, pltpu.HBM)
                       for x in (queries, stored_keys, stored_values)])

    return jax.shard_map(
        body,
        mesh=mesh,
        in_specs=(
            P(("grp", "kv"), None),
            P(("grp", "kv"), None),
            P(("grp", "kv"), None),
            P(("grp", "kv")),
        ),
        out_specs=P(("grp", "kv"), None),
        check_vma=False,
    )
```

```python
import functools
import math

import jax
import jax.numpy as jnp
from jax import lax
from jax.experimental import pallas as pl
from jax.experimental.pallas import tpu as pltpu
from jax.sharding import PartitionSpec as P

QUERY_HEADS = 64
KEY_VALUE_HEADS = 8
HEAD_DIM = 128
RATIO = QUERY_HEADS // KEY_VALUE_HEADS
FIRST = (0, 2, 6)
SIZE = (2, 4, 2)
PAIRS = len(SIZE)
TILE = 512
SCALE2 = HEAD_DIM ** (-0.5) * math.log2(math.e)
MESH = pl.DeviceIdType.MESH


def kernel(n, count_ref, q_hbm, k_hbm, v_hbm, out_ref,
           q_flat, q_rows, q_own, out_rows, k_buf, v_buf, q_buf,
           send_part, send_stat, pair_part, pair_stat,
           out_part, out_stat, out_row, recv_part, recv_row, s_buf,
           in_sem, kv_sem, q_recv, f_recv, x_recv, p_recv, s_recv, sent):
    me = lax.axis_index("kv")
    core = lax.rem(me, 2)
    chip = lax.div(me, 2)
    chips = n // 2
    sibling = me + 1 - 2 * core
    slots = k_buf.shape[1]
    block = min(chips, 8)

    def fetch(k):
        copies = []
        for g in range(FIRST[k], FIRST[k] + SIZE[k]):
            columns = pl.ds(g * HEAD_DIM, HEAD_DIM)
            copies.append(pltpu.make_async_copy(k_hbm.at[:, columns], k_buf.at[g], kv_sem.at[k]))
            copies.append(pltpu.make_async_copy(v_hbm.at[:, columns], v_buf.at[g], kv_sem.at[k]))
        return copies

    def rows(k):
        return pl.ds(FIRST[k] * RATIO, SIZE[k] * RATIO)

    def to(device, src, dst, send, recv):
        return pltpu.make_async_remote_copy(
            src_ref=src, dst_ref=dst, send_sem=send, recv_sem=recv,
            device_id={"kv": device}, device_id_type=MESH)

    def each_chip(body):
        def step(d, carry):
            other = lax.rem(chip + d, chips)
            body(other, 2 * other + core)
            return carry
        lax.fori_loop(1, chips, step, 0)

    def blocks(body):
        if chips == block:
            body(0)
        else:
            def step(b, carry):
                body(b)
                return carry
            lax.fori_loop(0, chips // block, step, 0)

    q_in = pltpu.make_async_copy(q_hbm, q_flat, in_sem.at[0])
    q_in.start()
    barrier = pltpu.get_barrier_semaphore()

    def signal(device):
        pl.semaphore_signal(barrier, inc=1, device_id={"kv": device}, device_id_type=MESH)

    each_chip(lambda other, device: signal(device))
    signal(sibling)
    for k in range(PAIRS):
        for copy in fetch(k):
            copy.start()

    q_in.wait()
    for h in range(QUERY_HEADS):
        q_rows[h:h + 1, :] = q_flat[:, h * HEAD_DIM:(h + 1) * HEAD_DIM].astype(jnp.float32)
    own = q_rows[...].astype(jnp.bfloat16)
    q_own[...] = own
    q_buf[core, chip] = own
    live = lax.broadcasted_iota(jnp.int32, (1, slots), 1) < count_ref[0]
    out_stat[...] = jnp.zeros_like(out_stat)
    pl.semaphore_wait(barrier, chips)

    for k in range(PAIRS):
        each_chip(lambda other, device: to(
            device, q_own.at[rows(k)], q_buf.at[core, chip, rows(k)],
            sent.at[0], q_recv.at[k]).start())

    def amount(part, sem):
        return pltpu.make_async_copy(part, part, sem)

    def forward(k):
        part = q_buf.at[core, :, rows(k)]
        return to(sibling, part, part, sent.at[0], f_recv.at[k])

    def swap_part(k):
        return to(sibling, send_part.at[1 - core, :, rows(k)], pair_part.at[:, rows(k)],
                  sent.at[0], x_recv.at[k])

    def swap_stat(k):
        return to(sibling, send_stat.at[1 - core, :, rows(k)], pair_stat.at[:, rows(k)],
                  sent.at[0], x_recv.at[k])

    def take(k):
        amount(q_buf.at[core, pl.ds(0, chips - 1), rows(k)], q_recv.at[k]).wait()
        forward(k).start()

    count = 2 * block * RATIO

    def compute(k):
        def one(b):
            group = pl.ds(b * block, block)
            parts = []
            stats = []
            peaks = []
            ones = jnp.ones((TILE, HEAD_DIM), jnp.bfloat16)
            for half in range(SIZE[k]):
                g = FIRST[k] + half
                q = q_buf[:, group, g * RATIO:(g + 1) * RATIO, :].astype(jnp.float32)
                q = q.reshape(count, HEAD_DIM).astype(jnp.bfloat16)
                peak = jnp.full((count, HEAD_DIM), -1e30, jnp.float32)
                for c in range(0, slots, TILE):
                    s = lax.dot_general(q, k_buf[g, c:c + TILE], (((1,), (1,)), ((), ())),
                                        preferred_element_type=jnp.float32)
                    s = jnp.where(live[:, c:c + TILE], s, -1e30)
                    s_buf[half, :, c:c + TILE] = s
                    for d in range(0, TILE, HEAD_DIM):
                        peak = jnp.maximum(peak, s[:, d:d + HEAD_DIM])
                peaks.append(jnp.max(peak, axis=1, keepdims=True) * SCALE2)
            for half in range(SIZE[k]):
                g = FIRST[k] + half
                top = peaks[half]
                o = jnp.zeros((count, 2 * HEAD_DIM), jnp.float32)
                for c in range(0, slots, TILE):
                    p = jnp.exp2(s_buf[half, :, c:c + TILE] * SCALE2 - top)
                    both = jnp.concatenate([v_buf[g, c:c + TILE], ones], axis=1)
                    o = o + jnp.dot(p.astype(jnp.bfloat16), both, preferred_element_type=jnp.float32)
                total = o[:, HEAD_DIM:]
                o = o[:, :HEAD_DIM]
                parts.append((o / total).reshape(2, block, RATIO, HEAD_DIM))
                stats.append((top + jnp.log2(total)).reshape(2, block, RATIO, HEAD_DIM))
            send_part[:, group, rows(k), :] = jnp.concatenate(parts, axis=2).astype(jnp.bfloat16)
            send_stat[:, group, rows(k), :] = jnp.concatenate(stats, axis=2)

        blocks(one)
        swap_part(k).start()
        swap_stat(k).start()

    shape = (block, RATIO, HEAD_DIM)
    lane = lax.broadcasted_iota(jnp.int32, shape, 2)
    row = lax.broadcasted_iota(jnp.int32, shape, 1)

    def merge(k):
        amount(send_stat.at[0, :, pl.ds(0, 3 * SIZE[k] * RATIO // 2)], x_recv.at[k]).wait()

        def one(b):
            group = pl.ds(b * block, block)
            a = send_part[core, group, rows(k), :].astype(jnp.float32)
            c = pair_part[group, rows(k), :].astype(jnp.float32)
            la = send_stat[core, group, rows(k), :]
            lc = pair_stat[group, rows(k), :]
            top = jnp.maximum(la, lc)
            wa = jnp.exp2(la - top)
            wc = jnp.exp2(lc - top)
            total = wa + wc
            out_part[group, rows(k), :] = ((wa * a + wc * c) / total).astype(jnp.bfloat16)
            lse = top + jnp.log2(total)
            stat = out_stat[group]
            for half in range(SIZE[k]):
                g = FIRST[k] + half
                stat = jnp.where(lane == g * RATIO + row, lse[:, half * RATIO:(half + 1) * RATIO, :], stat)
            if k < PAIRS - 1:
                out_stat[group] = stat
            else:
                out_row[group] = jnp.sum(stat, axis=1, keepdims=True)

        blocks(one)
        each_chip(lambda other, device: to(
            device, out_part.at[other, rows(k)], recv_part.at[chip, rows(k)],
            sent.at[0], p_recv.at[0]).start())
        if k == PAIRS - 1:
            each_chip(lambda other, device: to(
                device, out_row.at[other], recv_row.at[chip],
                sent.at[0], s_recv.at[0]).start())

    take(0)
    take(1)
    for k in range(PAIRS):
        forward(k).wait_recv()
        amount(k_buf.at[pl.ds(0, 2 * SIZE[k])], kv_sem.at[k]).wait()
        compute(k)
        if k + 2 < PAIRS:
            take(k + 2)
        if k > 0:
            merge(k - 1)
    merge(PAIRS - 1)
    recv_part[chip] = out_part[chip]
    recv_row[chip] = out_row[chip]

    others = pl.ds(0, chips - 1)
    amount(recv_part.at[others], p_recv.at[0]).wait()
    amount(recv_row.at[others], s_recv.at[0]).wait()

    lse = recv_row[...]
    weight = jnp.exp2(lse - jnp.max(lse, axis=0, keepdims=True))
    recv_row[...] = weight / jnp.sum(weight, axis=0, keepdims=True)
    lane2 = lax.broadcasted_iota(jnp.int32, (RATIO, HEAD_DIM), 1)
    row2 = lax.broadcasted_iota(jnp.int32, (RATIO, HEAD_DIM), 0)

    def add(j, acc):
        w = jnp.broadcast_to(recv_row[j], (RATIO, HEAD_DIM))
        x = recv_part[j].astype(jnp.float32)
        new = []
        for g in range(KEY_VALUE_HEADS):
            col = jnp.sum(jnp.where(lane2 == g * RATIO + row2, w, 0.0), axis=1, keepdims=True)
            new.append(acc[g] + col * x[g * RATIO:(g + 1) * RATIO, :])
        return tuple(new)

    zero = jnp.zeros((RATIO, HEAD_DIM), jnp.float32)
    acc = lax.fori_loop(0, chips, add, (zero,) * KEY_VALUE_HEADS, unroll=block)
    out_rows[...] = jnp.concatenate(acc, axis=0)
    for h in range(QUERY_HEADS):
        out_ref[:, h * HEAD_DIM:(h + 1) * HEAD_DIM] = out_rows[h:h + 1, :].astype(out_ref.dtype)

    amount(q_buf.at[0, others], sent.at[0]).wait()
    amount(q_buf.at[0], sent.at[0]).wait()
    amount(send_part.at[0], sent.at[0]).wait()
    amount(send_stat.at[0], sent.at[0]).wait()
    amount(recv_part.at[others], sent.at[0]).wait()
    amount(recv_row.at[others], sent.at[0]).wait()


def solution(mesh):
    n = mesh.shape["kv"]

    def body(queries, stored_keys, stored_values, kv_counts):
        slots = stored_keys.shape[0]
        chips = n // 2
        hbm = pl.BlockSpec(memory_space=pltpu.HBM)
        part = (chips, QUERY_HEADS, HEAD_DIM)
        both = (2,) + part
        dma = pltpu.SemaphoreType.DMA
        f32, b16 = jnp.float32, jnp.bfloat16
        return pl.pallas_call(
            functools.partial(kernel, n),
            out_shape=jax.ShapeDtypeStruct(queries.shape, b16),
            in_specs=[pl.BlockSpec(memory_space=pltpu.SMEM), hbm, hbm, hbm],
            out_specs=pl.BlockSpec(memory_space=pltpu.VMEM),
            scratch_shapes=[
                pltpu.VMEM(queries.shape, b16),
                pltpu.VMEM((QUERY_HEADS, HEAD_DIM), f32),
                pltpu.VMEM((QUERY_HEADS, HEAD_DIM), b16),
                pltpu.VMEM((QUERY_HEADS, HEAD_DIM), f32),
                pltpu.VMEM((KEY_VALUE_HEADS, slots, HEAD_DIM), b16),
                pltpu.VMEM((KEY_VALUE_HEADS, slots, HEAD_DIM), b16),
                pltpu.VMEM(both, b16),
                pltpu.VMEM(both, b16),
                pltpu.VMEM(both, f32),
                pltpu.VMEM(part, b16),
                pltpu.VMEM(part, f32),
                pltpu.VMEM(part, b16),
                pltpu.VMEM((chips, RATIO, HEAD_DIM), f32),
                pltpu.VMEM((chips, 1, HEAD_DIM), f32),
                pltpu.VMEM(part, b16),
                pltpu.VMEM((chips, 1, HEAD_DIM), f32),
                pltpu.VMEM((4, 2 * min(chips, 8) * RATIO, slots), f32),
                dma((1,)),
            ] + [dma((PAIRS,))] * 4 + [dma((1,))] * 3,
            compiler_params=pltpu.CompilerParams(
                collective_id=0, has_side_effects=True, vmem_limit_bytes=40 << 20),
        )(kv_counts, *[pltpu.with_memory_space_constraint(x, pltpu.HBM)
                       for x in (queries, stored_keys, stored_values)])

    return jax.shard_map(
        body,
        mesh=mesh,
        in_specs=(
            P(("grp", "kv"), None),
            P(("grp", "kv"), None),
            P(("grp", "kv"), None),
            P(("grp", "kv")),
        ),
        out_specs=P(("grp", "kv"), None),
        check_vma=False,
    )
```

```python
import functools
import math

import jax
import jax.numpy as jnp
from jax import lax
from jax.experimental import pallas as pl
from jax.experimental.pallas import tpu as pltpu
from jax.sharding import PartitionSpec as P

QUERY_HEADS = 64
KEY_VALUE_HEADS = 8
HEAD_DIM = 128
RATIO = QUERY_HEADS // KEY_VALUE_HEADS
FIRST = (0, 2, 6)
SIZE = (2, 4, 2)
PAIRS = len(SIZE)
NEAR = 3
TILE = 512
SCALE2 = HEAD_DIM ** (-0.5) * math.log2(math.e)
MESH = pl.DeviceIdType.MESH


def kernel(n, count_ref, q_hbm, k_hbm, v_hbm, out_ref,
           q_flat, q_rows, q_own, out_rows, k_buf, v_buf, q_buf,
           send_part, send_stat, pair_part, pair_stat,
           out_part, out_stat, out_row, recv_part, recv_row, s_buf,
           far_sem, in_sem, kv_sem, z_recv, q_recv, f_recv, x_recv, p_recv, s_recv, sent):
    me = lax.axis_index("kv")
    core = lax.rem(me, 2)
    chip = lax.div(me, 2)
    chips = n // 2
    sibling = me + 1 - 2 * core
    slots = k_buf.shape[1]
    block = min(chips, 8)

    def fetch(k):
        copies = []
        for g in range(FIRST[k], FIRST[k] + SIZE[k]):
            columns = pl.ds(g * HEAD_DIM, HEAD_DIM)
            copies.append(pltpu.make_async_copy(k_hbm.at[:, columns], k_buf.at[g], kv_sem.at[k]))
            copies.append(pltpu.make_async_copy(v_hbm.at[:, columns], v_buf.at[g], kv_sem.at[k]))
        return copies

    def rows(k):
        return pl.ds(FIRST[k] * RATIO, SIZE[k] * RATIO)

    def to(device, src, dst, send, recv):
        return pltpu.make_async_remote_copy(
            src_ref=src, dst_ref=dst, send_sem=send, recv_sem=recv,
            device_id={"kv": device}, device_id_type=MESH)

    def each_chip(body):
        def step(d, carry):
            other = lax.rem(chip + d, chips)
            body(other, 2 * other + core)
            return carry
        lax.fori_loop(1, chips, step, 0)

    def blocks(body):
        if chips == block:
            body(0)
        else:
            def step(b, carry):
                body(b)
                return carry
            lax.fori_loop(0, chips // block, step, 0)

    q_in = pltpu.make_async_copy(q_hbm, q_flat, in_sem.at[0])
    q_in.start()
    barrier = pltpu.get_barrier_semaphore()

    def signal(device):
        pl.semaphore_signal(barrier, inc=1, device_id={"kv": device}, device_id_type=MESH)

    end = chips - 1
    near = chip < NEAR
    last = chip == end

    signal(sibling)

    @pl.when(near)
    def _():
        signal(2 * end + 1 - core)

    @pl.when(jnp.logical_not(last))
    def _():
        each_chip(lambda other, device: signal(device))

    @pl.when(last)
    def _():
        pl.semaphore_wait(barrier, chips + NEAR)

        def greet(device):
            pl.semaphore_signal(far_sem, inc=1, device_id={"kv": device}, device_id_type=MESH)

        for device in range(2 * NEAR):
            greet(jnp.int32(device))

        def step(other, carry):
            greet(2 * other + core)
            return carry
        lax.fori_loop(NEAR, end, step, 0)

    for k in range(PAIRS):
        for copy in fetch(k):
            copy.start()

    q_in.wait()
    for h in range(QUERY_HEADS):
        q_rows[h:h + 1, :] = q_flat[:, h * HEAD_DIM:(h + 1) * HEAD_DIM].astype(jnp.float32)
    own = q_rows[...].astype(jnp.bfloat16)
    q_own[...] = own
    q_buf[core, chip] = own
    live = lax.broadcasted_iota(jnp.int32, (1, slots), 1) < count_ref[0]
    out_stat[...] = jnp.zeros_like(out_stat)
    def give(other, device, k, recv):
        to(device, q_own.at[rows(k)], q_buf.at[core, chip, rows(k)], sent.at[0], recv.at[k]).start()

    @pl.when(last)
    def _():
        for k in range(PAIRS):
            each_chip(lambda other, device: give(other, device, k, q_recv))

    @pl.when(jnp.logical_not(last))
    def _():
        pl.semaphore_wait(barrier, chips - 1)
        for k in range(PAIRS):
            def ahead(other, device):
                @pl.when(other != end)
                def _():
                    give(other, device, k, q_recv)
            each_chip(ahead)

        @pl.when(near)
        def _():
            pl.semaphore_wait(far_sem, 2)
            for k in range(PAIRS):
                for to_core in range(2):
                    give(end, 2 * end + to_core, k, z_recv)

        @pl.when(chip >= NEAR)
        def _():
            pl.semaphore_wait(far_sem, 1)
            for k in range(PAIRS):
                give(end, 2 * end + core, k, q_recv)

    def amount(part, sem):
        return pltpu.make_async_copy(part, part, sem)

    def across(k, start):
        part = q_buf.at[core, pl.ds(start, chips - start), rows(k)]
        return to(sibling, part, part, sent.at[0], f_recv.at[k])

    def take(k):
        @pl.when(last)
        def _():
            amount(q_buf.at[core, pl.ds(0, end - NEAR), rows(k)], q_recv.at[k]).wait()
            across(k, NEAR).start()

        @pl.when(jnp.logical_not(last))
        def _():
            amount(q_buf.at[core, pl.ds(0, chips - 1), rows(k)], q_recv.at[k]).wait()
            across(k, 0).start()

    def gathered(k):
        @pl.when(last)
        def _():
            across(k, NEAR).wait_recv()
            amount(q_buf.at[:, pl.ds(0, NEAR), rows(k)], z_recv.at[k]).wait()

        @pl.when(jnp.logical_not(last))
        def _():
            across(k, 0).wait_recv()

    def swap_part(k):
        return to(sibling, send_part.at[1 - core, :, rows(k)], pair_part.at[:, rows(k)],
                  sent.at[0], x_recv.at[k])

    def swap_stat(k):
        return to(sibling, send_stat.at[1 - core, :, rows(k)], pair_stat.at[:, rows(k)],
                  sent.at[0], x_recv.at[k])

    count = 2 * block * RATIO

    def compute(k):
        def one(b):
            group = pl.ds(b * block, block)
            parts = []
            stats = []
            peaks = []
            ones = jnp.ones((TILE, HEAD_DIM), jnp.bfloat16)
            for half in range(SIZE[k]):
                g = FIRST[k] + half
                q = q_buf[:, group, g * RATIO:(g + 1) * RATIO, :].astype(jnp.float32)
                q = q.reshape(count, HEAD_DIM).astype(jnp.bfloat16)
                peak = jnp.full((count, HEAD_DIM), -1e30, jnp.float32)
                for c in range(0, slots, TILE):
                    s = lax.dot_general(q, k_buf[g, c:c + TILE], (((1,), (1,)), ((), ())),
                                        preferred_element_type=jnp.float32)
                    s = jnp.where(live[:, c:c + TILE], s, -1e30)
                    s_buf[half, :, c:c + TILE] = s
                    for d in range(0, TILE, HEAD_DIM):
                        peak = jnp.maximum(peak, s[:, d:d + HEAD_DIM])
                peaks.append(jnp.max(peak, axis=1, keepdims=True) * SCALE2)
            for half in range(SIZE[k]):
                g = FIRST[k] + half
                top = peaks[half]
                o = jnp.zeros((count, 2 * HEAD_DIM), jnp.float32)
                for c in range(0, slots, TILE):
                    p = jnp.exp2(s_buf[half, :, c:c + TILE] * SCALE2 - top)
                    both = jnp.concatenate([v_buf[g, c:c + TILE], ones], axis=1)
                    o = o + jnp.dot(p.astype(jnp.bfloat16), both, preferred_element_type=jnp.float32)
                total = o[:, HEAD_DIM:]
                o = o[:, :HEAD_DIM]
                parts.append((o / total).reshape(2, block, RATIO, HEAD_DIM))
                stats.append((top + jnp.log2(total)).reshape(2, block, RATIO, HEAD_DIM))
            send_part[:, group, rows(k), :] = jnp.concatenate(parts, axis=2).astype(jnp.bfloat16)
            send_stat[:, group, rows(k), :] = jnp.concatenate(stats, axis=2)

        blocks(one)
        swap_part(k).start()
        swap_stat(k).start()

    shape = (block, RATIO, HEAD_DIM)
    lane = lax.broadcasted_iota(jnp.int32, shape, 2)
    row = lax.broadcasted_iota(jnp.int32, shape, 1)

    def merge(k):
        amount(send_stat.at[0, :, pl.ds(0, 3 * SIZE[k] * RATIO // 2)], x_recv.at[k]).wait()

        def one(b):
            group = pl.ds(b * block, block)
            a = send_part[core, group, rows(k), :].astype(jnp.float32)
            c = pair_part[group, rows(k), :].astype(jnp.float32)
            la = send_stat[core, group, rows(k), :]
            lc = pair_stat[group, rows(k), :]
            top = jnp.maximum(la, lc)
            wa = jnp.exp2(la - top)
            wc = jnp.exp2(lc - top)
            total = wa + wc
            out_part[group, rows(k), :] = ((wa * a + wc * c) / total).astype(jnp.bfloat16)
            lse = top + jnp.log2(total)
            stat = out_stat[group]
            for half in range(SIZE[k]):
                g = FIRST[k] + half
                stat = jnp.where(lane == g * RATIO + row, lse[:, half * RATIO:(half + 1) * RATIO, :], stat)
            if k < PAIRS - 1:
                out_stat[group] = stat
            else:
                out_row[group] = jnp.sum(stat, axis=1, keepdims=True)

        blocks(one)
        each_chip(lambda other, device: to(
            device, out_part.at[other, rows(k)], recv_part.at[chip, rows(k)],
            sent.at[0], p_recv.at[0]).start())
        if k == PAIRS - 1:
            each_chip(lambda other, device: to(
                device, out_row.at[other], recv_row.at[chip],
                sent.at[0], s_recv.at[0]).start())

    take(0)
    take(1)
    for k in range(PAIRS):
        gathered(k)
        amount(k_buf.at[pl.ds(0, 2 * SIZE[k])], kv_sem.at[k]).wait()
        compute(k)
        if k + 2 < PAIRS:
            take(k + 2)
        if k > 0:
            merge(k - 1)
    merge(PAIRS - 1)
    recv_part[chip] = out_part[chip]
    recv_row[chip] = out_row[chip]

    others = pl.ds(0, chips - 1)
    amount(recv_part.at[others], p_recv.at[0]).wait()
    amount(recv_row.at[others], s_recv.at[0]).wait()

    lse = recv_row[...]
    weight = jnp.exp2(lse - jnp.max(lse, axis=0, keepdims=True))
    recv_row[...] = weight / jnp.sum(weight, axis=0, keepdims=True)
    lane2 = lax.broadcasted_iota(jnp.int32, (RATIO, HEAD_DIM), 1)
    row2 = lax.broadcasted_iota(jnp.int32, (RATIO, HEAD_DIM), 0)

    def add(j, acc):
        w = jnp.broadcast_to(recv_row[j], (RATIO, HEAD_DIM))
        x = recv_part[j].astype(jnp.float32)
        new = []
        for g in range(KEY_VALUE_HEADS):
            col = jnp.sum(jnp.where(lane2 == g * RATIO + row2, w, 0.0), axis=1, keepdims=True)
            new.append(acc[g] + col * x[g * RATIO:(g + 1) * RATIO, :])
        return tuple(new)

    zero = jnp.zeros((RATIO, HEAD_DIM), jnp.float32)
    acc = lax.fori_loop(0, chips, add, (zero,) * KEY_VALUE_HEADS, unroll=block)
    out_rows[...] = jnp.concatenate(acc, axis=0)
    for h in range(QUERY_HEADS):
        out_ref[:, h * HEAD_DIM:(h + 1) * HEAD_DIM] = out_rows[h:h + 1, :].astype(out_ref.dtype)

    amount(q_buf.at[0, others], sent.at[0]).wait()

    @pl.when(last)
    def _():
        amount(q_buf.at[0, pl.ds(0, chips - NEAR)], sent.at[0]).wait()

    @pl.when(jnp.logical_not(last))
    def _():
        amount(q_buf.at[0], sent.at[0]).wait()

    @pl.when(near)
    def _():
        amount(q_buf.at[0, 0], sent.at[0]).wait()

    amount(send_part.at[0], sent.at[0]).wait()
    amount(send_stat.at[0], sent.at[0]).wait()
    amount(recv_part.at[others], sent.at[0]).wait()
    amount(recv_row.at[others], sent.at[0]).wait()


def solution(mesh):
    n = mesh.shape["kv"]

    def body(queries, stored_keys, stored_values, kv_counts):
        slots = stored_keys.shape[0]
        chips = n // 2
        hbm = pl.BlockSpec(memory_space=pltpu.HBM)
        part = (chips, QUERY_HEADS, HEAD_DIM)
        both = (2,) + part
        dma = pltpu.SemaphoreType.DMA
        f32, b16 = jnp.float32, jnp.bfloat16
        return pl.pallas_call(
            functools.partial(kernel, n),
            out_shape=jax.ShapeDtypeStruct(queries.shape, b16),
            in_specs=[pl.BlockSpec(memory_space=pltpu.SMEM), hbm, hbm, hbm],
            out_specs=pl.BlockSpec(memory_space=pltpu.VMEM),
            scratch_shapes=[
                pltpu.VMEM(queries.shape, b16),
                pltpu.VMEM((QUERY_HEADS, HEAD_DIM), f32),
                pltpu.VMEM((QUERY_HEADS, HEAD_DIM), b16),
                pltpu.VMEM((QUERY_HEADS, HEAD_DIM), f32),
                pltpu.VMEM((KEY_VALUE_HEADS, slots, HEAD_DIM), b16),
                pltpu.VMEM((KEY_VALUE_HEADS, slots, HEAD_DIM), b16),
                pltpu.VMEM(both, b16),
                pltpu.VMEM(both, b16),
                pltpu.VMEM(both, f32),
                pltpu.VMEM(part, b16),
                pltpu.VMEM(part, f32),
                pltpu.VMEM(part, b16),
                pltpu.VMEM((chips, RATIO, HEAD_DIM), f32),
                pltpu.VMEM((chips, 1, HEAD_DIM), f32),
                pltpu.VMEM(part, b16),
                pltpu.VMEM((chips, 1, HEAD_DIM), f32),
                pltpu.VMEM((4, 2 * min(chips, 8) * RATIO, slots), f32),
                pltpu.SemaphoreType.REGULAR,
                dma((1,)),
            ] + [dma((PAIRS,))] * 5 + [dma((1,))] * 3,
            compiler_params=pltpu.CompilerParams(
                collective_id=0, has_side_effects=True, vmem_limit_bytes=40 << 20),
        )(kv_counts, *[pltpu.with_memory_space_constraint(x, pltpu.HBM)
                       for x in (queries, stored_keys, stored_values)])

    return jax.shard_map(
        body,
        mesh=mesh,
        in_specs=(
            P(("grp", "kv"), None),
            P(("grp", "kv"), None),
            P(("grp", "kv"), None),
            P(("grp", "kv")),
        ),
        out_specs=P(("grp", "kv"), None),
        check_vma=False,
    )
```

```python
import functools
import math

import jax
import jax.numpy as jnp
from jax import lax
from jax.experimental import pallas as pl
from jax.experimental.pallas import tpu as pltpu
from jax.sharding import PartitionSpec as P

QUERY_HEADS = 64
KEY_VALUE_HEADS = 8
HEAD_DIM = 128
RATIO = QUERY_HEADS // KEY_VALUE_HEADS
FIRST = (0, 2, 6)
SIZE = (2, 4, 2)
PAIRS = len(SIZE)
NEAR = 3
TILE = 512
SCALE2 = HEAD_DIM ** (-0.5) * math.log2(math.e)
MESH = pl.DeviceIdType.MESH


def kernel(n, count_ref, q_hbm, k_hbm, v_hbm, out_ref,
           q_flat, q_rows, q_own, out_rows, k_buf, v_buf, q_buf,
           send_part, send_stat, pair_part, pair_stat,
           out_part, out_stat, out_row, recv_part, recv_row, s_buf,
           far_sem, in_sem, kv_sem, z_recv, q_recv, f_recv, x_recv, p_recv, s_recv, sent):
    me = lax.axis_index("kv")
    core = lax.rem(me, 2)
    chip = lax.div(me, 2)
    chips = n // 2
    sibling = me + 1 - 2 * core
    slots = k_buf.shape[1]
    block = min(chips, 8)

    def fetch(k):
        copies = []
        for g in range(FIRST[k], FIRST[k] + SIZE[k]):
            columns = pl.ds(g * HEAD_DIM, HEAD_DIM)
            copies.append(pltpu.make_async_copy(k_hbm.at[:, columns], k_buf.at[g], kv_sem.at[k]))
            copies.append(pltpu.make_async_copy(v_hbm.at[:, columns], v_buf.at[g], kv_sem.at[k]))
        return copies

    def rows(k):
        return pl.ds(FIRST[k] * RATIO, SIZE[k] * RATIO)

    def to(device, src, dst, send, recv):
        return pltpu.make_async_remote_copy(
            src_ref=src, dst_ref=dst, send_sem=send, recv_sem=recv,
            device_id={"kv": device}, device_id_type=MESH)

    def each_chip(body):
        def step(d, carry):
            other = lax.rem(chip + d, chips)
            body(other, 2 * other + core)
            return carry
        lax.fori_loop(1, chips, step, 0)

    def blocks(body):
        if chips == block:
            body(0)
        else:
            def step(b, carry):
                body(b)
                return carry
            lax.fori_loop(0, chips // block, step, 0)

    q_in = pltpu.make_async_copy(q_hbm, q_flat, in_sem.at[0])
    q_in.start()
    barrier = pltpu.get_barrier_semaphore()

    def signal(device):
        pl.semaphore_signal(barrier, inc=1, device_id={"kv": device}, device_id_type=MESH)

    end = chips - 1
    near = chip < NEAR
    last = chip == end

    signal(sibling)

    @pl.when(near)
    def _():
        signal(2 * end + 1 - core)

    @pl.when(jnp.logical_not(last))
    def _():
        each_chip(lambda other, device: signal(device))

    @pl.when(last)
    def _():
        pl.semaphore_wait(barrier, chips + NEAR)

        def greet(device):
            pl.semaphore_signal(far_sem, inc=1, device_id={"kv": device}, device_id_type=MESH)

        for device in range(2 * NEAR):
            greet(jnp.int32(device))

        def step(other, carry):
            greet(2 * other + core)
            return carry
        lax.fori_loop(NEAR, end, step, 0)

    for k in range(PAIRS):
        for copy in fetch(k):
            copy.start()

    q_in.wait()
    for h in range(QUERY_HEADS):
        q_rows[h:h + 1, :] = q_flat[:, h * HEAD_DIM:(h + 1) * HEAD_DIM].astype(jnp.float32)
    own = q_rows[...].astype(jnp.bfloat16)
    q_own[...] = own
    q_buf[core, chip] = own
    live = lax.broadcasted_iota(jnp.int32, (1, slots), 1) < count_ref[0]
    out_stat[...] = jnp.zeros_like(out_stat)
    def give(other, device, k, recv):
        to(device, q_own.at[rows(k)], q_buf.at[core, chip, rows(k)], sent.at[0], recv.at[k]).start()

    @pl.when(last)
    def _():
        for k in range(PAIRS):
            each_chip(lambda other, device: give(other, device, k, q_recv))

    @pl.when(jnp.logical_not(last))
    def _():
        pl.semaphore_wait(barrier, chips - 1)
        for k in range(PAIRS):
            def ahead(other, device):
                @pl.when(other != end)
                def _():
                    give(other, device, k, q_recv)
            each_chip(ahead)

        @pl.when(near)
        def _():
            pl.semaphore_wait(far_sem, 2)
            for k in range(PAIRS):
                for to_core in range(2):
                    give(end, 2 * end + to_core, k, z_recv)

        @pl.when(chip >= NEAR)
        def _():
            pl.semaphore_wait(far_sem, 1)
            for k in range(PAIRS):
                give(end, 2 * end + core, k, q_recv)

    def amount(part, sem):
        return pltpu.make_async_copy(part, part, sem)

    def across(k, start):
        part = q_buf.at[core, pl.ds(start, chips - start), rows(k)]
        return to(sibling, part, part, sent.at[0], f_recv.at[k])

    def take(k):
        @pl.when(last)
        def _():
            amount(q_buf.at[core, pl.ds(0, end - NEAR), rows(k)], q_recv.at[k]).wait()
            across(k, NEAR).start()

        @pl.when(jnp.logical_not(last))
        def _():
            amount(q_buf.at[core, pl.ds(0, chips - 1), rows(k)], q_recv.at[k]).wait()
            across(k, 0).start()

    def gathered(k):
        @pl.when(last)
        def _():
            across(k, NEAR).wait_recv()
            amount(q_buf.at[:, pl.ds(0, NEAR), rows(k)], z_recv.at[k]).wait()

        @pl.when(jnp.logical_not(last))
        def _():
            across(k, 0).wait_recv()

    def swap_part(k):
        return to(sibling, send_part.at[1 - core, :, rows(k)], pair_part.at[:, rows(k)],
                  sent.at[0], x_recv.at[k])

    def swap_stat(k):
        return to(sibling, send_stat.at[1 - core, :, rows(k)], pair_stat.at[:, rows(k)],
                  sent.at[0], x_recv.at[k])

    count = 2 * block * RATIO

    def compute(k):
        def one(b):
            group = pl.ds(b * block, block)
            parts = []
            stats = []
            peaks = []
            ones = jnp.ones((TILE, HEAD_DIM), jnp.bfloat16)
            for half in range(SIZE[k]):
                g = FIRST[k] + half
                q = q_buf[:, group, g * RATIO:(g + 1) * RATIO, :].astype(jnp.float32)
                q = q.reshape(count, HEAD_DIM).astype(jnp.bfloat16)
                peak = jnp.full((count, HEAD_DIM), -1e30, jnp.float32)
                for c in range(0, slots, TILE):
                    s = lax.dot_general(q, k_buf[g, c:c + TILE], (((1,), (1,)), ((), ())),
                                        preferred_element_type=jnp.float32)
                    s = jnp.where(live[:, c:c + TILE], s, -1e30)
                    s_buf[half, :, c:c + TILE] = s
                    for d in range(0, TILE, HEAD_DIM):
                        peak = jnp.maximum(peak, s[:, d:d + HEAD_DIM])
                peaks.append(jnp.max(peak, axis=1, keepdims=True) * SCALE2)
            for half in range(SIZE[k]):
                g = FIRST[k] + half
                top = peaks[half]
                o = jnp.zeros((count, 2 * HEAD_DIM), jnp.float32)
                for c in range(0, slots, TILE):
                    p = jnp.exp2(s_buf[half, :, c:c + TILE] * SCALE2 - top)
                    both = jnp.concatenate([v_buf[g, c:c + TILE], ones], axis=1)
                    o = o + jnp.dot(p.astype(jnp.bfloat16), both, preferred_element_type=jnp.float32)
                total = o[:, HEAD_DIM:]
                o = o[:, :HEAD_DIM]
                parts.append((o / total).reshape(2, block, RATIO, HEAD_DIM))
                stats.append((top + jnp.log2(total)).reshape(2, block, RATIO, HEAD_DIM))
            send_part[:, group, rows(k), :] = jnp.concatenate(parts, axis=2).astype(jnp.bfloat16)
            send_stat[:, group, rows(k), :] = jnp.concatenate(stats, axis=2)

        blocks(one)
        swap_part(k).start()
        swap_stat(k).start()

    shape = (block, RATIO, HEAD_DIM)
    lane = lax.broadcasted_iota(jnp.int32, shape, 2)
    row = lax.broadcasted_iota(jnp.int32, shape, 1)

    def merge(k):
        amount(send_stat.at[0, :, pl.ds(0, 3 * SIZE[k] * RATIO // 2)], x_recv.at[k]).wait()

        def one(b):
            group = pl.ds(b * block, block)
            a = send_part[core, group, rows(k), :].astype(jnp.float32)
            c = pair_part[group, rows(k), :].astype(jnp.float32)
            la = send_stat[core, group, rows(k), :]
            lc = pair_stat[group, rows(k), :]
            top = jnp.maximum(la, lc)
            wa = jnp.exp2(la - top)
            wc = jnp.exp2(lc - top)
            total = wa + wc
            out_part[group, rows(k), :] = ((wa * a + wc * c) / total).astype(jnp.bfloat16)
            lse = top + jnp.log2(total)
            stat = out_stat[group]
            for half in range(SIZE[k]):
                g = FIRST[k] + half
                stat = jnp.where(lane == g * RATIO + row, lse[:, half * RATIO:(half + 1) * RATIO, :], stat)
            if k < PAIRS - 1:
                out_stat[group] = stat
            else:
                out_row[group] = jnp.sum(stat, axis=1, keepdims=True)

        blocks(one)
        def deliver(other, device):
            to(device, out_part.at[other, rows(k)], recv_part.at[chip, rows(k)],
               sent.at[0], p_recv.at[0]).start()
            if k == PAIRS - 1:
                to(device, out_row.at[other], recv_row.at[chip], sent.at[0], s_recv.at[0]).start()

        each_chip(deliver)

    take(0)
    take(1)
    for k in range(PAIRS):
        gathered(k)
        amount(k_buf.at[pl.ds(0, 2 * SIZE[k])], kv_sem.at[k]).wait()
        compute(k)
        if k + 2 < PAIRS:
            take(k + 2)
        if k > 0:
            merge(k - 1)
    merge(PAIRS - 1)
    recv_part[chip] = out_part[chip]
    recv_row[chip] = out_row[chip]

    others = pl.ds(0, chips - 1)
    amount(recv_part.at[others], p_recv.at[0]).wait()
    amount(recv_row.at[others], s_recv.at[0]).wait()

    lse = recv_row[...]
    weight = jnp.exp2(lse - jnp.max(lse, axis=0, keepdims=True))
    recv_row[...] = weight / jnp.sum(weight, axis=0, keepdims=True)
    lane2 = lax.broadcasted_iota(jnp.int32, (RATIO, HEAD_DIM), 1)
    row2 = lax.broadcasted_iota(jnp.int32, (RATIO, HEAD_DIM), 0)

    def add(j, acc):
        w = jnp.broadcast_to(recv_row[j], (RATIO, HEAD_DIM))
        x = recv_part[j].astype(jnp.float32)
        new = []
        for g in range(KEY_VALUE_HEADS):
            col = jnp.sum(jnp.where(lane2 == g * RATIO + row2, w, 0.0), axis=1, keepdims=True)
            new.append(acc[g] + col * x[g * RATIO:(g + 1) * RATIO, :])
        return tuple(new)

    zero = jnp.zeros((RATIO, HEAD_DIM), jnp.float32)
    acc = lax.fori_loop(0, chips, add, (zero,) * KEY_VALUE_HEADS, unroll=block)
    out_rows[...] = jnp.concatenate(acc, axis=0)
    for h in range(QUERY_HEADS):
        out_ref[:, h * HEAD_DIM:(h + 1) * HEAD_DIM] = out_rows[h:h + 1, :].astype(out_ref.dtype)

    amount(q_buf.at[0, others], sent.at[0]).wait()

    @pl.when(last)
    def _():
        amount(q_buf.at[0, pl.ds(0, chips - NEAR)], sent.at[0]).wait()

    @pl.when(jnp.logical_not(last))
    def _():
        amount(q_buf.at[0], sent.at[0]).wait()

    @pl.when(near)
    def _():
        amount(q_buf.at[0, 0], sent.at[0]).wait()

    amount(send_part.at[0], sent.at[0]).wait()
    amount(send_stat.at[0], sent.at[0]).wait()
    amount(recv_part.at[others], sent.at[0]).wait()
    amount(recv_row.at[others], sent.at[0]).wait()


def solution(mesh):
    n = mesh.shape["kv"]

    def body(queries, stored_keys, stored_values, kv_counts):
        slots = stored_keys.shape[0]
        chips = n // 2
        hbm = pl.BlockSpec(memory_space=pltpu.HBM)
        part = (chips, QUERY_HEADS, HEAD_DIM)
        both = (2,) + part
        dma = pltpu.SemaphoreType.DMA
        f32, b16 = jnp.float32, jnp.bfloat16
        return pl.pallas_call(
            functools.partial(kernel, n),
            out_shape=jax.ShapeDtypeStruct(queries.shape, b16),
            in_specs=[pl.BlockSpec(memory_space=pltpu.SMEM), hbm, hbm, hbm],
            out_specs=pl.BlockSpec(memory_space=pltpu.VMEM),
            scratch_shapes=[
                pltpu.VMEM(queries.shape, b16),
                pltpu.VMEM((QUERY_HEADS, HEAD_DIM), f32),
                pltpu.VMEM((QUERY_HEADS, HEAD_DIM), b16),
                pltpu.VMEM((QUERY_HEADS, HEAD_DIM), f32),
                pltpu.VMEM((KEY_VALUE_HEADS, slots, HEAD_DIM), b16),
                pltpu.VMEM((KEY_VALUE_HEADS, slots, HEAD_DIM), b16),
                pltpu.VMEM(both, b16),
                pltpu.VMEM(both, b16),
                pltpu.VMEM(both, f32),
                pltpu.VMEM(part, b16),
                pltpu.VMEM(part, f32),
                pltpu.VMEM(part, b16),
                pltpu.VMEM((chips, RATIO, HEAD_DIM), f32),
                pltpu.VMEM((chips, 1, HEAD_DIM), f32),
                pltpu.VMEM(part, b16),
                pltpu.VMEM((chips, 1, HEAD_DIM), f32),
                pltpu.VMEM((4, 2 * min(chips, 8) * RATIO, slots), f32),
                pltpu.SemaphoreType.REGULAR,
                dma((1,)),
            ] + [dma((PAIRS,))] * 5 + [dma((1,))] * 3,
            compiler_params=pltpu.CompilerParams(
                collective_id=0, has_side_effects=True, vmem_limit_bytes=40 << 20),
        )(kv_counts, *[pltpu.with_memory_space_constraint(x, pltpu.HBM)
                       for x in (queries, stored_keys, stored_values)])

    return jax.shard_map(
        body,
        mesh=mesh,
        in_specs=(
            P(("grp", "kv"), None),
            P(("grp", "kv"), None),
            P(("grp", "kv"), None),
            P(("grp", "kv")),
        ),
        out_specs=P(("grp", "kv"), None),
        check_vma=False,
    )
```
